32 devices in a mesh: row: 8 (over z, y), col: 4 (over x, core).
Axes of the slice: x: 2, y: 2, z: 4, core: 2. Of those that a mesh axis runs over, the one named last changes fastest.
Arguments:
- matrix: float32 [6144, 16384], P('row', 'col'), may hold values from -6 to 6
Outputs:
- updated: float32 [6144, 16384], P('row', 'col')
The draws below stay inside these ranges and needn't reach their ends.
All inputs are finite; a program needn't handle non-finite values.
Results may differ from the reference program's by a relative error of at most 0.0003.
Values sent between devices are 32-bit elements; how exact they have to be, the bound alone decides.
A program may use at most 128 MiB of HBM per device.

```python
import jax
import jax.numpy as jnp
from jax import lax

PANEL = 128
N = 16384
M = 6144


def block_scale(rng, dims, split, least, high):
    loudness, own = 1.0, jax.random.fold_in(rng, 6)
    for axis_at, shards_of in split:
        steps = jnp.exp(jax.random.uniform(jax.random.fold_in(own, axis_at), (shards_of,), jnp.float32, least / len(split), high / len(split)))
        loudness = loudness * jnp.repeat(steps, dims[axis_at] // shards_of).reshape([-1 if axis == axis_at else 1 for axis in range(len(dims))])
    return loudness


def gaussian(own_key, extent, spread, most, cuts=(), kind=jnp.bfloat16):
    drawn = jax.random.normal(own_key, extent, jnp.float32) * spread
    if len(cuts) > 0:
        drawn = block_scale(own_key, extent, cuts, -0.22, 0.18) * drawn
    return jnp.clip(drawn, min=-most, max=most).astype(kind)


def setup_inputs(seed: int = 0) -> dict:
    key_list = jax.random.split(jax.random.key(seed), 2)
    matrix = gaussian(key_list[0], (M, N), 1.0, 6.0, ((0, 8), (1, 4)), jnp.float32)
    return dict(matrix=matrix)


def eliminate(working):
    count = working.shape[0]
    positions = jnp.arange(count).astype(jnp.int32)

    def one_column(column, state):
        pivot_value = state[column, column]
        below = positions > column
        multiplier = jnp.where(below, state[:, column] / pivot_value, jnp.zeros_like(state[:, column]))
        pivot_row = jnp.where(below, state[column, :], jnp.zeros_like(state[column, :]))
        state = state - multiplier[:, None] * pivot_row[None, :]
        return state.at[:, column].set(jnp.where(below, multiplier, state[:, column]))
    result = lax.fori_loop(0, count, one_column, working)
    lower_unit = jnp.tril(result, -1) + jnp.eye(count, dtype=result.dtype)
    upper_tri = jnp.triu(result)
    return (lower_unit, upper_tri)

def reference(matrix):
    high = lax.Precision.HIGHEST
    panel_cols = matrix[:, :PANEL]
    orthonormal, triangle = jnp.linalg.qr(panel_cols)
    sign_fix = jnp.sign(jnp.diagonal(triangle))
    orthonormal = orthonormal * sign_fix[None, :]
    lower_unit, upper_tri = eliminate(orthonormal[:PANEL] + jnp.eye(PANEL, dtype=jnp.float32))
    reflectors = jax.scipy.linalg.solve_triangular(upper_tri.T, orthonormal.T, lower=True)
    reflectors = reflectors.at[:, :PANEL].set(lower_unit.T)
    projected = jnp.dot(reflectors, matrix, precision=high)
    coefficients = jax.scipy.linalg.solve_triangular(lower_unit, jnp.dot(upper_tri.T, projected, precision=high), lower=True, unit_diagonal=True)
    return matrix - jnp.dot(reflectors.T, coefficients, precision=high)
```

```python
import jax
import jax.numpy as jnp
from jax import lax
from jax.experimental import pallas as pl
from jax.experimental.pallas import tpu as pltpu
from jax.sharding import PartitionSpec as P

PANEL = 128
STRIP = 8


def dot_exact(a, b, contract):
    return lax.dot_general(
        a, b, (contract, ((), ())), precision=lax.Precision.HIGHEST, preferred_element_type=jnp.float32
    )


def factor_values(gram, top):
    strips = PANEL // STRIP
    rows = lax.broadcasted_iota(jnp.int32, (STRIP, 1), 0)
    eye = (
        lax.broadcasted_iota(jnp.int32, (PANEL, PANEL), 0) == lax.broadcasted_iota(jnp.int32, (PANEL, PANEL), 1)
    ).astype(jnp.float32)
    chol = jnp.concatenate([gram, eye], axis=1)
    work = jnp.concatenate([top, jnp.zeros_like(top)], axis=1)
    factor_rows = []
    for strip in range(strips):
        at = strip * STRIP
        panel = chol[:STRIP]
        scale = jnp.ones((STRIP, 1), jnp.float32)
        for j in range(STRIP):
            column = panel[:, at + j : at + j + 1]
            pivot = column[j : j + 1]
            multiplier = jnp.where(rows > j, column / pivot, 0.0)
            scale = jnp.where(rows == j, lax.rsqrt(pivot), scale)
            panel = panel - multiplier * panel[j : j + 1]
        panel = panel * scale
        lanes = lax.broadcasted_iota(jnp.int32, (STRIP, 2 * PANEL), 1)
        panel = jnp.where(lanes >= at + rows, panel, 0.0)
        factor_rows.append(panel[:, :PANEL])
        if strip < strips - 1:
            below = panel[:, at + STRIP : PANEL]
            chol = chol[STRIP:] - dot_exact(below, panel, ((0,), (0,)))

        inner = work[at : at + STRIP] + panel
        for j in range(STRIP):
            column = inner[:, at + j : at + j + 1]
            pivot_row = inner[j : j + 1] / column[j : j + 1]
            inner = jnp.where(rows == j, pivot_row, inner - column * pivot_row)
        update = dot_exact(work[:, at : at + STRIP], inner, ((1,), (0,)))
        pieces = []
        if at > 0:
            pieces.append(work[:at] - update[:at])
        pieces.append(inner)
        if strip < strips - 1:
            pieces.append(work[at + STRIP :] - update[at + STRIP :])
        work = jnp.concatenate(pieces, axis=0)
    return jnp.concatenate(factor_rows, axis=0), work[:, PANEL:]


def factor_kernel(gram_ref, top_ref, factor_ref, inverse_ref):
    factor, inverse = factor_values(gram_ref[...], top_ref[...])
    factor_ref[...] = factor
    inverse_ref[...] = inverse


def factorize(gram, top):
    square = jax.ShapeDtypeStruct((PANEL, PANEL), jnp.float32)
    return pl.pallas_call(factor_kernel, out_shape=(square, square), name="factorize")(gram, top)


def on_device(matrix):
    own = jnp.where(lax.axis_index("col") == 0, matrix[:, :PANEL], 0.0)
    panel = lax.psum(own, "col")
    first = lax.axis_index("row") == 0
    gram_part = jnp.dot(panel.T, panel, precision=lax.Precision.HIGHEST)
    gram, top = lax.psum((gram_part, jnp.where(first, panel[:PANEL], 0.0)), "row")
    factor, inverse = factorize(gram, top)
    shifted = panel.at[:PANEL].add(jnp.where(first, factor, 0.0))
    partial = lax.dot_general(shifted, matrix, (((0,), (0,)), ((), ())), precision=lax.Precision.HIGH)
    summed = lax.psum(partial, "row")
    coefficients = jnp.dot(inverse, summed, precision=lax.Precision.HIGH)
    return matrix - jnp.dot(shifted, coefficients, precision=lax.Precision.HIGH)


def solution(mesh):
    return jax.shard_map(
        on_device, mesh=mesh, in_specs=(P("row", "col"),), out_specs=P("row", "col"), check_vma=False
    )
```

```python
import functools

import jax
import jax.numpy as jnp
from jax import lax
from jax.experimental import pallas as pl
from jax.experimental.pallas import tpu as pltpu
from jax.sharding import PartitionSpec as P

PANEL = 128
STRIP = 8
LANES = 128
MESH = pl.DeviceIdType.MESH


def dot_exact(a, b, contract):
    return lax.dot_general(
        a, b, (contract, ((), ())), precision=lax.Precision.HIGHEST, preferred_element_type=jnp.float32
    )


def factor_values(gram, top):
    strips = PANEL // STRIP
    rows = lax.broadcasted_iota(jnp.int32, (STRIP, 1), 0)
    eye = (
        lax.broadcasted_iota(jnp.int32, (PANEL, PANEL), 0) == lax.broadcasted_iota(jnp.int32, (PANEL, PANEL), 1)
    ).astype(jnp.float32)
    chol = jnp.concatenate([gram, eye], axis=1)
    work = jnp.concatenate([top, jnp.zeros_like(top)], axis=1)
    factor_rows = []
    for strip in range(strips):
        at = strip * STRIP
        panel = chol[:STRIP]
        scale = jnp.ones((STRIP, 1), jnp.float32)
        for j in range(STRIP):
            column = panel[:, at + j : at + j + 1]
            pivot = column[j : j + 1]
            multiplier = jnp.where(rows > j, column / pivot, 0.0)
            scale = jnp.where(rows == j, lax.rsqrt(pivot), scale)
            panel = panel - multiplier * panel[j : j + 1]
        panel = panel * scale
        lanes = lax.broadcasted_iota(jnp.int32, (STRIP, 2 * PANEL), 1)
        panel = jnp.where(lanes >= at + rows, panel, 0.0)
        factor_rows.append(panel[:, :PANEL])
        if strip < strips - 1:
            below = panel[:, at + STRIP : PANEL]
            chol = chol[STRIP:] - dot_exact(below, panel, ((0,), (0,)))

        inner = work[at : at + STRIP] + panel
        for j in range(STRIP):
            column = inner[:, at + j : at + j + 1]
            pivot_row = inner[j : j + 1] / column[j : j + 1]
            inner = jnp.where(rows == j, pivot_row, inner - column * pivot_row)
        update = dot_exact(work[:, at : at + STRIP], inner, ((1,), (0,)))
        pieces = []
        if at > 0:
            pieces.append(work[:at] - update[:at])
        pieces.append(inner)
        if strip < strips - 1:
            pieces.append(work[at + STRIP :] - update[at + STRIP :])
        work = jnp.concatenate(pieces, axis=0)
    return jnp.concatenate(factor_rows, axis=0), work[:, PANEL:]


def factor_kernel(gram_ref, top_ref, factor_ref, inverse_ref):
    factor, inverse = factor_values(gram_ref[...], top_ref[...])
    factor_ref[...] = factor
    inverse_ref[...] = inverse


def factorize(gram, top):
    square = jax.ShapeDtypeStruct((PANEL, PANEL), jnp.float32)
    return pl.pallas_call(factor_kernel, out_shape=(square, square), name="factorize")(gram, top)


def everyone_ready(n_row, n_col):
    row, col = lax.axis_index("row"), lax.axis_index("col")
    barrier = pltpu.get_barrier_semaphore()
    for d in range(1, n_row):
        pl.semaphore_signal(barrier, inc=1, device_id={"row": lax.rem(row + d, n_row)}, device_id_type=MESH)
    for d in range(1, n_col):
        pl.semaphore_signal(barrier, inc=1, device_id={"col": lax.rem(col + d, n_col)}, device_id_type=MESH)
    pl.semaphore_wait(barrier, n_row - 1 + max(n_col - 1, 0))


def send(src, dst, send_sem, recv_sem, target):
    return pltpu.make_async_remote_copy(
        src_ref=src, dst_ref=dst, send_sem=send_sem, recv_sem=recv_sem, device_id=target, device_id_type=MESH
    )


def front_kernel(
    n_row, n_col, matrix_ref, panel_out, gram_out, top_out,
    panel, top, parts, arrived, whole, local_sem, panel_send, top_send, part_send, whole_send, share_send,
    panel_recv, top_recv, part_recv, whole_recv, share_recv,
):
    row, col = lax.axis_index("row"), lax.axis_index("col")
    piece = PANEL // n_row
    everyone_ready(n_row, n_col)

    @pl.when(col == 0)
    def _():
        fetch = pltpu.make_async_copy(matrix_ref.at[:, pl.ds(0, PANEL)], panel, local_sem.at[0])
        fetch.start()
        fetch.wait()
        panel_copies = [
            send(panel, panel, panel_send.at[c - 1], panel_recv.at[0], {"col": c}) for c in range(1, n_col)
        ]

        @pl.when(row == 0)
        def _():
            for r in range(1, n_row):
                send(panel.at[pl.ds(0, PANEL)], top, top_send.at[r - 1], top_recv.at[0], {"row": r}).start()
            own = pltpu.make_async_copy(panel.at[pl.ds(0, PANEL)], top, local_sem.at[1])
            own.start()
            own.wait()

        local = dot_exact(panel[...], panel[...], ((0,), (0,)))
        for q in range(n_row):
            parts[q] = local[q * piece : (q + 1) * piece]
        part_copies = []
        for d in range(1, n_row):
            q = lax.rem(row + d, n_row)
            part_copies.append(
                send(parts.at[q], arrived.at[d - 1], part_send.at[d - 1], part_recv.at[d - 1], {"row": q})
            )
            part_copies[-1].start()
        for copy in panel_copies:
            copy.start()
        total = parts[row]
        for d in range(1, n_row):
            part_copies[d - 1].wait_recv()
            total = total + arrived[d - 1]
        whole[row] = total
        whole_copies = []
        for d in range(1, n_row):
            q = lax.rem(row + d, n_row)
            whole_copies.append(
                send(whole.at[row], whole.at[row], whole_send.at[d - 1], whole_recv.at[d - 1], {"row": q})
            )
            whole_copies[-1].start()

        @pl.when(row != 0)
        def _():
            send(top, top, top_send.at[0], top_recv.at[0], {"row": 0}).wait_recv()

        for d in range(1, n_row):
            q = lax.rem(row - d + n_row, n_row)
            send(whole.at[q], whole.at[q], whole_send.at[d - 1], whole_recv.at[d - 1], {"row": q}).wait_recv()
        shares = []
        for c in range(1, n_col):
            shares.append(send(top, top, share_send.at[2 * c - 2], share_recv.at[0], {"col": c}))
            shares.append(send(whole, whole, share_send.at[2 * c - 1], share_recv.at[1], {"col": c}))
        for copy in shares:
            copy.start()

        @pl.when(row == 0)
        def _():
            for r in range(1, n_row):
                send(panel.at[pl.ds(0, PANEL)], top, top_send.at[r - 1], top_recv.at[0], {"row": r}).wait_send()

        for copy in part_copies + panel_copies + whole_copies + shares:
            copy.wait_send()

    @pl.when(col != 0)
    def _():
        root = {"col": 0}
        send(panel, panel, panel_send.at[0], panel_recv.at[0], root).wait_recv()
        send(top, top, share_send.at[0], share_recv.at[0], root).wait_recv()
        send(whole, whole, share_send.at[1], share_recv.at[1], root).wait_recv()

    panel_out[...] = panel[...]
    top_out[...] = top[...]
    for q in range(n_row):
        gram_out[q * piece : (q + 1) * piece] = whole[q]


def front(matrix, n_row, n_col):
    height = matrix.shape[0]
    piece = PANEL // n_row
    dma = pltpu.SemaphoreType.DMA
    square = jax.ShapeDtypeStruct((PANEL, PANEL), jnp.float32)
    return pl.pallas_call(
        functools.partial(front_kernel, n_row, n_col),
        out_shape=(jax.ShapeDtypeStruct((height, PANEL), jnp.float32), square, square),
        in_specs=[pl.BlockSpec(memory_space=pl.ANY)],
        out_specs=(pl.BlockSpec(memory_space=pltpu.VMEM),) * 3,
        scratch_shapes=[
            pltpu.VMEM((height, PANEL), jnp.float32),
            pltpu.VMEM((PANEL, PANEL), jnp.float32),
            pltpu.VMEM((n_row, piece, PANEL), jnp.float32),
            pltpu.VMEM((n_row - 1, piece, PANEL), jnp.float32),
            pltpu.VMEM((n_row, piece, PANEL), jnp.float32),
            dma((2,)),
            dma((n_col - 1,)),
            dma((n_row - 1,)),
            dma((n_row - 1,)),
            dma((n_row - 1,)),
            dma((2 * n_col - 2,)),
            dma((1,)),
            dma((1,)),
            dma((n_row - 1,)),
            dma((n_row - 1,)),
            dma((2,)),
        ],
        compiler_params=pltpu.CompilerParams(collective_id=0, has_side_effects=True),
        name="front",
    )(matrix)


def sum_kernel(
    n_row, inner_n, chunks, part_ref, out_ref,
    pair_in, half, far_in, hold, pair_send, far_send, done_send, back_send, pair_recv, far_recv, done_recv, back_recv,
):
    row = lax.axis_index("row")
    outer_n = n_row // inner_n
    outer, inner = row // inner_n, lax.rem(row, inner_n)
    other = 1 - inner
    partner = {"row": outer * inner_n + other}
    span = outer_n * LANES
    everyone_ready(n_row, 1)

    def columns(k, i):
        return pl.ds(pl.multiple_of((k * inner_n + i) * span, span), span)

    def peer(d):
        return lax.rem(outer + d, outer_n)

    def pair(k):
        return send(part_ref.at[:, columns(k, other)], pair_in.at[k], pair_send.at[k], pair_recv.at[k], partner)

    def far(k, d):
        q = peer(d)
        return send(
            half.at[k, q], far_in.at[k, d - 1], far_send.at[k, d - 1], far_recv.at[k, d - 1],
            {"row": q * inner_n + inner},
        )

    def spot(k, o):
        return pl.ds(pl.multiple_of((k * inner_n + inner) * span + o * LANES, LANES), LANES)

    def done(k, d):
        return send(
            hold.at[:, spot(k, outer)], hold.at[:, spot(k, outer)], done_send.at[k, d - 1], done_recv.at[k, d - 1],
            {"row": peer(d) * inner_n + inner},
        )

    def back(k):
        return send(hold.at[:, columns(k, inner)], hold.at[:, columns(k, inner)], back_send.at[k], back_recv.at[k], partner)

    def stage_far(k):
        pair(k).wait_recv()
        for o in range(outer_n):
            place = pl.ds(pl.multiple_of((k * inner_n + inner) * span + o * LANES, LANES), LANES)
            half[k, o] = part_ref[:, place] + pair_in[k, :, o * LANES : (o + 1) * LANES]
        for d in range(1, outer_n):
            far(k, d).start()

    def stage_done(k):
        total = half[k, outer]
        for d in range(1, outer_n):
            far(k, d).wait_recv()
            total = total + far_in[k, d - 1]
        hold[:, spot(k, outer)] = total
        for d in range(1, outer_n):
            done(k, d).start()

    def stage_back(k):
        for d in range(1, outer_n):
            q = lax.rem(outer - d + outer_n, outer_n)
            send(
                hold.at[:, spot(k, q)], hold.at[:, spot(k, q)], done_send.at[k, d - 1], done_recv.at[k, d - 1],
                {"row": q * inner_n + inner},
            ).wait_recv()
        back(k).start()

    for k in range(chunks):
        pair(k).start()
    for step in range(chunks + 2):
        if step < chunks:
            stage_far(step)
        if 0 <= step - 1 < chunks:
            stage_done(step - 1)
        if 0 <= step - 2 < chunks:
            stage_back(step - 2)
    for k in range(chunks):
        mirror = hold.at[:, columns(k, other)]
        send(mirror, mirror, back_send.at[k], back_recv.at[k], partner).wait_recv()
    for k in range(chunks):
        pair(k).wait_send()
        back(k).wait_send()
        for d in range(1, outer_n):
            far(k, d).wait_send()
            done(k, d).wait_send()
    out_ref[...] = hold[...]


def sum_rows(part, n_row):
    width = part.shape[1]
    inner_n = 2
    outer_n = n_row // inner_n
    chunks = width // (n_row * LANES)
    span = outer_n * LANES
    dma = pltpu.SemaphoreType.DMA
    return pl.pallas_call(
        functools.partial(sum_kernel, n_row, inner_n, chunks),
        out_shape=jax.ShapeDtypeStruct(part.shape, jnp.float32),
        in_specs=[pl.BlockSpec(memory_space=pltpu.VMEM)],
        out_specs=pl.BlockSpec(memory_space=pltpu.VMEM),
        scratch_shapes=[
            pltpu.VMEM((chunks, PANEL, span), jnp.float32),
            pltpu.VMEM((chunks, outer_n, PANEL, LANES), jnp.float32),
            pltpu.VMEM((chunks, outer_n - 1, PANEL, LANES), jnp.float32),
            pltpu.VMEM((PANEL, width), jnp.float32),
            dma((chunks,)),
            dma((chunks, outer_n - 1)),
            dma((chunks, outer_n - 1)),
            dma((chunks,)),
            dma((chunks,)),
            dma((chunks, outer_n - 1)),
            dma((chunks, outer_n - 1)),
            dma((chunks,)),
        ],
        compiler_params=pltpu.CompilerParams(collective_id=1, has_side_effects=True),
        name="sum_rows",
    )(part)


def on_device(n_row, n_col, matrix):
    panel, gram, top = front(matrix, n_row, n_col)
    first = lax.axis_index("row") == 0
    factor, inverse = factorize(gram, top)
    shifted = panel.at[:PANEL].add(jnp.where(first, factor, 0.0))
    partial = lax.dot_general(shifted, matrix, (((0,), (0,)), ((), ())), precision=lax.Precision.HIGH)
    summed = sum_rows(partial, n_row)
    coefficients = jnp.dot(inverse, summed, precision=lax.Precision.HIGH)
    return matrix - jnp.dot(shifted, coefficients, precision=lax.Precision.HIGH)


def solution(mesh):
    body = functools.partial(on_device, mesh.shape["row"], mesh.shape["col"])
    return jax.shard_map(body, mesh=mesh, in_specs=(P("row", "col"),), out_specs=P("row", "col"), check_vma=False)
```

```python
import functools

import jax
import jax.numpy as jnp
from jax import lax
from jax.experimental import pallas as pl
from jax.experimental.pallas import tpu as pltpu
from jax.sharding import PartitionSpec as P

PANEL = 128
STRIP = 8
LANES = 128
MESH = pl.DeviceIdType.MESH


def dot_exact(a, b, contract):
    return lax.dot_general(
        a, b, (contract, ((), ())), precision=lax.Precision.HIGHEST, preferred_element_type=jnp.float32
    )


def factor_values(gram, top, between=lambda strip: None):
    strips = PANEL // STRIP
    rows = lax.broadcasted_iota(jnp.int32, (STRIP, 1), 0)
    eye = (
        lax.broadcasted_iota(jnp.int32, (PANEL, PANEL), 0) == lax.broadcasted_iota(jnp.int32, (PANEL, PANEL), 1)
    ).astype(jnp.float32)
    chol = jnp.concatenate([gram, eye], axis=1)
    work = jnp.concatenate([top, jnp.zeros_like(top)], axis=1)
    factor_rows = []
    for strip in range(strips):
        between(strip)
        at = strip * STRIP
        panel = chol[:STRIP]
        scale = jnp.ones((STRIP, 1), jnp.float32)
        for j in range(STRIP):
            column = panel[:, at + j : at + j + 1]
            pivot = column[j : j + 1]
            multiplier = jnp.where(rows > j, column / pivot, 0.0)
            scale = jnp.where(rows == j, lax.rsqrt(pivot), scale)
            panel = panel - multiplier * panel[j : j + 1]
        panel = panel * scale
        lanes = lax.broadcasted_iota(jnp.int32, (STRIP, 2 * PANEL), 1)
        panel = jnp.where(lanes >= at + rows, panel, 0.0)
        factor_rows.append(panel[:, :PANEL])
        if strip < strips - 1:
            below = panel[:, at + STRIP : PANEL]
            chol = chol[STRIP:] - dot_exact(below, panel, ((0,), (0,)))

        inner = work[at : at + STRIP] + panel
        for j in range(STRIP):
            column = inner[:, at + j : at + j + 1]
            pivot_row = inner[j : j + 1] / column[j : j + 1]
            inner = jnp.where(rows == j, pivot_row, inner - column * pivot_row)
        update = dot_exact(work[:, at : at + STRIP], inner, ((1,), (0,)))
        pieces = []
        if at > 0:
            pieces.append(work[:at] - update[:at])
        pieces.append(inner)
        if strip < strips - 1:
            pieces.append(work[at + STRIP :] - update[at + STRIP :])
        work = jnp.concatenate(pieces, axis=0)
    return jnp.concatenate(factor_rows, axis=0), work[:, PANEL:]


def everyone_ready(n_row, n_col):
    row, col = lax.axis_index("row"), lax.axis_index("col")
    barrier = pltpu.get_barrier_semaphore()
    for d in range(1, n_row):
        pl.semaphore_signal(barrier, inc=1, device_id={"row": lax.rem(row + d, n_row)}, device_id_type=MESH)
    for d in range(1, n_col):
        pl.semaphore_signal(barrier, inc=1, device_id={"col": lax.rem(col + d, n_col)}, device_id_type=MESH)
    pl.semaphore_wait(barrier, n_row - 1 + max(n_col - 1, 0))


def send(src, dst, send_sem, recv_sem, target):
    return pltpu.make_async_remote_copy(
        src_ref=src, dst_ref=dst, send_sem=send_sem, recv_sem=recv_sem, device_id=target, device_id_type=MESH
    )


def split(x):
    high = x.astype(jnp.bfloat16)
    return high, (x - high.astype(jnp.float32)).astype(jnp.bfloat16)


def step_kernel(
    n_row, n_col, inner_n, chunks, matrix_ref, shifted_out, hold,
    block, partial, stacked, pair_in, half, far_in, top_in, panel, top, parts, arrived, whole,
    local_sem, block_sem, own_sem,
    panel_send, top_send, part_send, whole_send, share_send, scatter_send,
    panel_recv, top_recv, part_recv, whole_recv, share_recv, scatter_recv,
    pair_send, far_send, done_send, back_send, pair_recv, far_recv, done_recv, back_recv,
):
    row, col = lax.axis_index("row"), lax.axis_index("col")
    piece = PANEL // n_row
    outer_n = n_row // inner_n
    outer, inner = row // inner_n, lax.rem(row, inner_n)
    other = 1 - inner
    partner = {"row": outer * inner_n + other}
    span = outer_n * LANES
    everyone_ready(n_row, n_col)

    def load(k):
        place = pl.ds(k * inner_n * span, inner_n * span)
        return pltpu.make_async_copy(matrix_ref.at[:, place], block.at[:, place], block_sem.at[k])

    def scatter(k, r):
        place = pl.ds((k * inner_n + r % inner_n) * span + r // inner_n * LANES, LANES)
        return send(
            matrix_ref.at[pl.ds(0, PANEL), place], top_in.at[k],
            scatter_send.at[k, r - 1], scatter_recv.at[k], {"row": r},
        )

    def keep(k):
        place = pl.ds(k * inner_n * span, LANES)
        return pltpu.make_async_copy(matrix_ref.at[pl.ds(0, PANEL), place], top_in.at[k], own_sem.at[k])

    def start_scatter():
        for k in range(chunks):
            for r in range(1, n_row):
                scatter(k, r).start()
            keep(k).start()

    @pl.when((row == 0) & (col != 0))
    def _():
        start_scatter()

    @pl.when(col == 0)
    def _():
        fetch = pltpu.make_async_copy(matrix_ref.at[:, pl.ds(0, PANEL)], panel, local_sem.at[0])
        fetch.start()
        fetch.wait()
        for k in range(chunks):
            load(k).start()
        panel_copies = [
            send(panel, panel, panel_send.at[c - 1], panel_recv.at[0], {"col": c}) for c in range(1, n_col)
        ]

        @pl.when(row == 0)
        def _():
            for r in range(1, n_row):
                send(panel.at[pl.ds(0, PANEL)], top, top_send.at[r - 1], top_recv.at[0], {"row": r}).start()
            own = pltpu.make_async_copy(panel.at[pl.ds(0, PANEL)], top, local_sem.at[1])
            own.start()
            own.wait()

        local = dot_exact(panel[...], panel[...], ((0,), (0,)))
        for q in range(n_row):
            parts[q] = local[q * piece : (q + 1) * piece]
        part_copies = []
        for d in range(1, n_row):
            q = lax.rem(row + d, n_row)
            part_copies.append(
                send(parts.at[q], arrived.at[d - 1], part_send.at[d - 1], part_recv.at[d - 1], {"row": q})
            )
            part_copies[-1].start()
        for copy in panel_copies:
            copy.start()
        total = parts[row]
        for d in range(1, n_row):
            part_copies[d - 1].wait_recv()
            total = total + arrived[d - 1]
        whole[row] = total
        whole_copies = []
        for d in range(1, n_row):
            q = lax.rem(row + d, n_row)
            whole_copies.append(
                send(whole.at[row], whole.at[row], whole_send.at[d - 1], whole_recv.at[d - 1], {"row": q})
            )
            whole_copies[-1].start()

        @pl.when(row != 0)
        def _():
            send(top, top, top_send.at[0], top_recv.at[0], {"row": 0}).wait_recv()

        for d in range(1, n_row):
            q = lax.rem(row - d + n_row, n_row)
            send(whole.at[q], whole.at[q], whole_send.at[d - 1], whole_recv.at[d - 1], {"row": q}).wait_recv()
        shares = []
        for c in range(1, n_col):
            shares.append(send(top, top, share_send.at[2 * c - 2], share_recv.at[0], {"col": c}))
            shares.append(send(whole, whole, share_send.at[2 * c - 1], share_recv.at[1], {"col": c}))
        for copy in shares:
            copy.start()

        @pl.when(row == 0)
        def _():
            for r in range(1, n_row):
                send(panel.at[pl.ds(0, PANEL)], top, top_send.at[r - 1], top_recv.at[0], {"row": r}).wait_send()

        for copy in part_copies + panel_copies + whole_copies + shares:
            copy.wait_send()

    @pl.when(col != 0)
    def _():
        for k in range(chunks):
            load(k).start()
        root = {"col": 0}
        send(panel, panel, panel_send.at[0], panel_recv.at[0], root).wait_recv()
        send(top, top, share_send.at[0], share_recv.at[0], root).wait_recv()
        send(whole, whole, share_send.at[1], share_recv.at[1], root).wait_recv()

    @pl.when((row == 0) & (col == 0))
    def _():
        start_scatter()

    def columns(k, i):
        return pl.ds(pl.multiple_of((k * inner_n + i) * span, span), span)

    def peer(d):
        return lax.rem(outer + d, outer_n)

    def pair(k):
        return send(partial.at[:, columns(k, other)], pair_in.at[k], pair_send.at[k], pair_recv.at[k], partner)

    def far(k, d):
        q = peer(d)
        return send(
            half.at[k, q], far_in.at[k, d - 1], far_send.at[k, d - 1], far_recv.at[k, d - 1],
            {"row": q * inner_n + inner},
        )

    def spot(k, o):
        return pl.ds(pl.multiple_of((k * inner_n + inner) * span + o * LANES, LANES), LANES)

    def done(k, d):
        return send(
            hold.at[:, spot(k, outer)], hold.at[:, spot(k, outer)], done_send.at[k, d - 1], done_recv.at[k, d - 1],
            {"row": peer(d) * inner_n + inner},
        )

    def back(k):
        return send(hold.at[:, columns(k, inner)], hold.at[:, columns(k, inner)], back_send.at[k], back_recv.at[k], partner)

    def multiply(k, i):
        place = columns(k, i)
        high, low = split(block[:, place])
        both = jnp.dot(stacked[...], high, preferred_element_type=jnp.float32)
        rest = jnp.dot(stacked[:PANEL], low, preferred_element_type=jnp.float32)
        partial[:, place] = both[:PANEL] + both[PANEL:] + rest

    def stage_far(k):
        pair(k).wait_recv()
        for o in range(outer_n):
            half[k, o] = partial[:, spot(k, o)] + pair_in[k, :, o * LANES : (o + 1) * LANES]
        for d in range(1, outer_n):
            far(k, d).start()

    def stage_done(k, factor, inverse):
        total = half[k, outer]
        for d in range(1, outer_n):
            far(k, d).wait_recv()
            total = total + far_in[k, d - 1]

        @pl.when(row == 0)
        def _():
            keep(k).wait()

        @pl.when(row != 0)
        def _():
            send(top_in.at[k], top_in.at[k], scatter_send.at[k, 0], scatter_recv.at[k], {"row": 0}).wait_recv()

        total = total + dot_exact(factor, top_in[k], ((0,), (0,)))
        hold[:, spot(k, outer)] = dot_exact(inverse, total, ((1,), (0,)))
        for d in range(1, outer_n):
            done(k, d).start()

    def stage_back(k):
        for d in range(1, outer_n):
            q = lax.rem(outer - d + outer_n, outer_n)
            send(
                hold.at[:, spot(k, q)], hold.at[:, spot(k, q)], done_send.at[k, d - 1], done_recv.at[k, d - 1],
                {"row": q * inner_n + inner},
            ).wait_recv()
        back(k).start()

    for k in range(chunks):
        load(k).wait()
    high, low = split(jnp.transpose(panel[...]))
    stacked[:PANEL] = high
    stacked[PANEL:] = low
    gram = jnp.concatenate([whole[q] for q in range(n_row)], axis=0)

    def between(strip):
        if strip < chunks:
            multiply(strip, other)
            pair(strip).start()
        elif strip < 2 * chunks:
            multiply(strip - chunks, inner)
        elif strip >= 2 * chunks + 2 and strip % 2 == 0 and (strip - 2 * chunks - 2) // 2 < chunks - 1:
            stage_far((strip - 2 * chunks - 2) // 2)

    ready = max(0, min(chunks - 1, (PANEL // STRIP - 2 * chunks - 1) // 2))
    factor, inverse = factor_values(gram, top[...], between)
    for step in range(chunks + 2):
        if step < ready:
            stage_done(step, factor, inverse)
        if ready + step < chunks:
            stage_far(ready + step)
        if ready <= step < chunks:
            stage_done(step, factor, inverse)
        if 0 <= step - 2 < chunks:
            stage_back(step - 2)
    shifted_out[...] = panel[...]

    @pl.when(row == 0)
    def _():
        shifted_out[:PANEL] = panel[:PANEL] + factor
        for k in range(chunks):
            for r in range(1, n_row):
                scatter(k, r).wait_send()

    for k in range(chunks):
        mirror = hold.at[:, columns(k, other)]
        send(mirror, mirror, back_send.at[k], back_recv.at[k], partner).wait_recv()
    for k in range(chunks):
        pair(k).wait_send()
        back(k).wait_send()
        for d in range(1, outer_n):
            far(k, d).wait_send()
            done(k, d).wait_send()


def whole_step(matrix, n_row, n_col):
    height, width = matrix.shape
    piece = PANEL // n_row
    inner_n = 2
    outer_n = n_row // inner_n
    chunks = width // (n_row * LANES)
    span = outer_n * LANES
    dma = pltpu.SemaphoreType.DMA
    f32 = jnp.float32
    return pl.pallas_call(
        functools.partial(step_kernel, n_row, n_col, inner_n, chunks),
        out_shape=(jax.ShapeDtypeStruct((height, PANEL), f32), jax.ShapeDtypeStruct((PANEL, width), f32)),
        in_specs=[pl.BlockSpec(memory_space=pl.ANY)],
        out_specs=(pl.BlockSpec(memory_space=pltpu.VMEM),) * 2,
        scratch_shapes=[
            pltpu.VMEM((height, width), f32),
            pltpu.VMEM((PANEL, width), f32),
            pltpu.VMEM((2 * PANEL, height), jnp.bfloat16),
            pltpu.VMEM((chunks, PANEL, span), f32),
            pltpu.VMEM((chunks, outer_n, PANEL, LANES), f32),
            pltpu.VMEM((chunks, outer_n - 1, PANEL, LANES), f32),
            pltpu.VMEM((chunks, PANEL, LANES), f32),
            pltpu.VMEM((height, PANEL), f32),
            pltpu.VMEM((PANEL, PANEL), f32),
            pltpu.VMEM((n_row, piece, PANEL), f32),
            pltpu.VMEM((n_row - 1, piece, PANEL), f32),
            pltpu.VMEM((n_row, piece, PANEL), f32),
            dma((2,)),
            dma((chunks,)),
            dma((chunks,)),
            dma((n_col - 1,)),
            dma((n_row - 1,)),
            dma((n_row - 1,)),
            dma((n_row - 1,)),
            dma((2 * n_col - 2,)),
            dma((chunks, n_row - 1)),
            dma((1,)),
            dma((1,)),
            dma((n_row - 1,)),
            dma((n_row - 1,)),
            dma((2,)),
            dma((chunks,)),
            dma((chunks,)),
            dma((chunks, outer_n - 1)),
            dma((chunks, outer_n - 1)),
            dma((chunks,)),
            dma((chunks,)),
            dma((chunks, outer_n - 1)),
            dma((chunks, outer_n - 1)),
            dma((chunks,)),
        ],
        compiler_params=pltpu.CompilerParams(
            collective_id=0, has_side_effects=True, vmem_limit_bytes=48 * 1024 * 1024
        ),
        name="whole_step",
    )(matrix)


def on_device(n_row, n_col, matrix):
    shifted, coefficients = whole_step(matrix, n_row, n_col)
    return matrix - jnp.dot(shifted, coefficients, precision=lax.Precision.HIGH)


def solution(mesh):
    body = functools.partial(on_device, mesh.shape["row"], mesh.shape["col"])
    return jax.shard_map(body, mesh=mesh, in_specs=(P("row", "col"),), out_specs=P("row", "col"), check_vma=False)
```

```python
import functools

import jax
import jax.numpy as jnp
from jax import lax
from jax.experimental import pallas as pl
from jax.experimental.pallas import tpu as pltpu
from jax.sharding import PartitionSpec as P

PANEL = 128
STRIP = 8
LANES = 128
MESH = pl.DeviceIdType.MESH


def dot_exact(a, b, contract):
    return lax.dot_general(
        a, b, (contract, ((), ())), precision=lax.Precision.HIGHEST, preferred_element_type=jnp.float32
    )


def factor_values(gram, top, between=lambda strip: None):
    strips = PANEL // STRIP
    rows = lax.broadcasted_iota(jnp.int32, (STRIP, 1), 0)
    eye = (
        lax.broadcasted_iota(jnp.int32, (PANEL, PANEL), 0) == lax.broadcasted_iota(jnp.int32, (PANEL, PANEL), 1)
    ).astype(jnp.float32)
    chol = jnp.concatenate([gram, eye], axis=1)
    work = jnp.concatenate([top, jnp.zeros_like(top)], axis=1)
    factor_rows = []
    lanes = lax.broadcasted_iota(jnp.int32, (STRIP, 2 * PANEL), 1)
    previous = None
    for strip in range(strips + 1):
        at, back = strip * STRIP, (strip - 1) * STRIP
        if strip < strips:
            between(strip)
            panel = chol[:STRIP]
            scale = jnp.ones((STRIP, 1), jnp.float32)
        if strip > 0:
            inner = work[back : back + STRIP] + previous
            aside = work[:, back : back + STRIP]
        for j in range(STRIP):
            if strip < strips:
                column = panel[:, at + j : at + j + 1]
                pivot = column[j : j + 1]
                multiplier = jnp.where(rows > j, column / pivot, 0.0)
            if strip > 0:
                inner_column = inner[:, back + j : back + j + 1]
                pivot_row = inner[j : j + 1] / inner_column[j : j + 1]
            if strip < strips:
                scale = jnp.where(rows == j, lax.rsqrt(pivot), scale)
                panel = panel - multiplier * panel[j : j + 1]
            if strip > 0:
                inner = jnp.where(rows == j, pivot_row, inner - inner_column * pivot_row)
        if strip < strips:
            panel = jnp.where(lanes >= at + rows, panel * scale, 0.0)
            factor_rows.append(panel[:, :PANEL])
            if strip < strips - 1:
                chol = chol[STRIP:] - dot_exact(panel[:, at + STRIP : PANEL], panel, ((0,), (0,)))
        if strip > 0:
            update = dot_exact(aside, inner, ((1,), (0,)))
            pieces = []
            if back > 0:
                pieces.append(work[:back] - update[:back])
            pieces.append(inner)
            if strip < strips:
                pieces.append(work[at:] - update[at:])
            work = jnp.concatenate(pieces, axis=0)
        previous = panel
    return jnp.concatenate(factor_rows, axis=0), work[:, PANEL:]


def everyone_ready(n_row, n_col):
    row, col = lax.axis_index("row"), lax.axis_index("col")
    barrier = pltpu.get_barrier_semaphore()
    for d in range(1, n_row):
        pl.semaphore_signal(barrier, inc=1, device_id={"row": lax.rem(row + d, n_row)}, device_id_type=MESH)
    for d in range(1, n_col):
        pl.semaphore_signal(barrier, inc=1, device_id={"col": lax.rem(col + d, n_col)}, device_id_type=MESH)
    pl.semaphore_wait(barrier, n_row - 1 + max(n_col - 1, 0))


def send(src, dst, send_sem, recv_sem, target):
    return pltpu.make_async_remote_copy(
        src_ref=src, dst_ref=dst, send_sem=send_sem, recv_sem=recv_sem, device_id=target, device_id_type=MESH
    )


def split(x):
    high = x.astype(jnp.bfloat16)
    return high, (x - high.astype(jnp.float32)).astype(jnp.bfloat16)


def step_kernel(
    n_row, n_col, inner_n, chunks, matrix_ref, shifted_out, hold,
    block, partial, stacked, pair_in, half, far_in, top_in, panel, top, parts, arrived, whole,
    local_sem, block_sem, own_sem,
    panel_send, top_send, part_send, whole_send, share_send, scatter_send,
    panel_recv, top_recv, part_recv, whole_recv, share_recv, scatter_recv,
    pair_send, far_send, done_send, back_send, pair_recv, far_recv, done_recv, back_recv,
):
    row, col = lax.axis_index("row"), lax.axis_index("col")
    piece = PANEL // n_row
    outer_n = n_row // inner_n
    outer, inner = row // inner_n, lax.rem(row, inner_n)
    other = 1 - inner
    partner = {"row": outer * inner_n + other}
    span = outer_n * LANES
    everyone_ready(n_row, n_col)

    def load(k):
        place = pl.ds(k * inner_n * span, inner_n * span)
        return pltpu.make_async_copy(matrix_ref.at[:, place], block.at[:, place], block_sem.at[k])

    def scatter(k, r):
        place = pl.ds((k * inner_n + r % inner_n) * span + r // inner_n * LANES, LANES)
        return send(
            matrix_ref.at[pl.ds(0, PANEL), place], top_in.at[k],
            scatter_send.at[k, r - 1], scatter_recv.at[k], {"row": r},
        )

    def keep(k):
        place = pl.ds(k * inner_n * span, LANES)
        return pltpu.make_async_copy(matrix_ref.at[pl.ds(0, PANEL), place], top_in.at[k], own_sem.at[k])

    def start_scatter():
        for k in range(chunks):
            for r in range(1, n_row):
                scatter(k, r).start()
            keep(k).start()

    @pl.when((row == 0) & (col != 0))
    def _():
        start_scatter()

    @pl.when(col == 0)
    def _():
        fetch = pltpu.make_async_copy(matrix_ref.at[:, pl.ds(0, PANEL)], panel, local_sem.at[0])
        fetch.start()
        fetch.wait()
        for k in range(chunks):
            load(k).start()
        panel_copies = [
            send(panel, panel, panel_send.at[c - 1], panel_recv.at[0], {"col": c}) for c in range(1, n_col)
        ]

        @pl.when(row == 0)
        def _():
            for r in range(1, n_row):
                send(panel.at[pl.ds(0, PANEL)], top, top_send.at[r - 1], top_recv.at[0], {"row": r}).start()
            own = pltpu.make_async_copy(panel.at[pl.ds(0, PANEL)], top, local_sem.at[1])
            own.start()
            own.wait()

        local = dot_exact(panel[...], panel[...], ((0,), (0,)))
        for q in range(n_row):
            parts[q] = local[q * piece : (q + 1) * piece]
        part_copies = []
        for d in range(1, n_row):
            q = lax.rem(row + d, n_row)
            part_copies.append(
                send(parts.at[q], arrived.at[d - 1], part_send.at[d - 1], part_recv.at[d - 1], {"row": q})
            )
            part_copies[-1].start()
        for copy in panel_copies:
            copy.start()
        total = parts[row]
        for d in range(1, n_row):
            part_copies[d - 1].wait_recv()
            total = total + arrived[d - 1]
        whole[row] = total
        whole_copies = []
        for d in range(1, n_row):
            q = lax.rem(row + d, n_row)
            whole_copies.append(
                send(whole.at[row], whole.at[row], whole_send.at[d - 1], whole_recv.at[d - 1], {"row": q})
            )
            whole_copies[-1].start()

        @pl.when(row != 0)
        def _():
            send(top, top, top_send.at[0], top_recv.at[0], {"row": 0}).wait_recv()

        for d in range(1, n_row):
            q = lax.rem(row - d + n_row, n_row)
            send(whole.at[q], whole.at[q], whole_send.at[d - 1], whole_recv.at[d - 1], {"row": q}).wait_recv()
        shares = []
        for c in range(1, n_col):
            shares.append(send(top, top, share_send.at[2 * c - 2], share_recv.at[0], {"col": c}))
            shares.append(send(whole, whole, share_send.at[2 * c - 1], share_recv.at[1], {"col": c}))
        for copy in shares:
            copy.start()

        @pl.when(row == 0)
        def _():
            for r in range(1, n_row):
                send(panel.at[pl.ds(0, PANEL)], top, top_send.at[r - 1], top_recv.at[0], {"row": r}).wait_send()

        for copy in part_copies + panel_copies + whole_copies + shares:
            copy.wait_send()

    @pl.when(col != 0)
    def _():
        for k in range(chunks):
            load(k).start()
        root = {"col": 0}
        send(panel, panel, panel_send.at[0], panel_recv.at[0], root).wait_recv()
        send(top, top, share_send.at[0], share_recv.at[0], root).wait_recv()
        send(whole, whole, share_send.at[1], share_recv.at[1], root).wait_recv()

    @pl.when((row == 0) & (col == 0))
    def _():
        start_scatter()

    def columns(k, i):
        return pl.ds(pl.multiple_of((k * inner_n + i) * span, span), span)

    def peer(d):
        return lax.rem(outer + d, outer_n)

    def pair(k):
        return send(partial.at[:, columns(k, other)], pair_in.at[k], pair_send.at[k], pair_recv.at[k], partner)

    def far(k, d):
        q = peer(d)
        return send(
            half.at[k, q], far_in.at[k, d - 1], far_send.at[k, d - 1], far_recv.at[k, d - 1],
            {"row": q * inner_n + inner},
        )

    def spot(k, o):
        return pl.ds(pl.multiple_of((k * inner_n + inner) * span + o * LANES, LANES), LANES)

    def done(k, d):
        return send(
            hold.at[:, spot(k, outer)], hold.at[:, spot(k, outer)], done_send.at[k, d - 1], done_recv.at[k, d - 1],
            {"row": peer(d) * inner_n + inner},
        )

    def back(k):
        return send(hold.at[:, columns(k, inner)], hold.at[:, columns(k, inner)], back_send.at[k], back_recv.at[k], partner)

    def multiply(k, i):
        place = columns(k, i)
        high, low = split(block[:, place])
        both = jnp.dot(stacked[...], high, preferred_element_type=jnp.float32)
        rest = jnp.dot(stacked[:PANEL], low, preferred_element_type=jnp.float32)
        partial[:, place] = both[:PANEL] + both[PANEL:] + rest

    def stage_far(k):
        pair(k).wait_recv()
        for o in range(outer_n):
            half[k, o] = partial[:, spot(k, o)] + pair_in[k, :, o * LANES : (o + 1) * LANES]
        for d in range(1, outer_n):
            far(k, d).start()

    def stage_done(k, factor, inverse):
        total = half[k, outer]
        for d in range(1, outer_n):
            far(k, d).wait_recv()
            total = total + far_in[k, d - 1]

        @pl.when(row == 0)
        def _():
            keep(k).wait()

        @pl.when(row != 0)
        def _():
            send(top_in.at[k], top_in.at[k], scatter_send.at[k, 0], scatter_recv.at[k], {"row": 0}).wait_recv()

        total = total + dot_exact(factor, top_in[k], ((0,), (0,)))
        hold[:, spot(k, outer)] = dot_exact(inverse, total, ((1,), (0,)))
        for d in range(1, outer_n):
            done(k, d).start()

    def stage_back(k):
        for d in range(1, outer_n):
            q = lax.rem(outer - d + outer_n, outer_n)
            send(
                hold.at[:, spot(k, q)], hold.at[:, spot(k, q)], done_send.at[k, d - 1], done_recv.at[k, d - 1],
                {"row": q * inner_n + inner},
            ).wait_recv()
        back(k).start()

    for k in range(chunks):
        load(k).wait()
    high, low = split(jnp.transpose(panel[...]))
    stacked[:PANEL] = high
    stacked[PANEL:] = low
    gram = jnp.concatenate([whole[q] for q in range(n_row)], axis=0)

    def between(strip):
        if strip < chunks:
            multiply(strip, other)
            pair(strip).start()
        elif strip < 2 * chunks:
            multiply(strip - chunks, inner)
        elif strip >= 2 * chunks + 2 and strip % 2 == 0 and (strip - 2 * chunks - 2) // 2 < chunks - 1:
            stage_far((strip - 2 * chunks - 2) // 2)

    ready = max(0, min(chunks - 1, (PANEL // STRIP - 2 * chunks - 1) // 2))
    factor, inverse = factor_values(gram, top[...], between)
    for step in range(chunks + 2):
        if step < ready:
            stage_done(step, factor, inverse)
        if ready + step < chunks:
            stage_far(ready + step)
        if ready <= step < chunks:
            stage_done(step, factor, inverse)
        if 0 <= step - 2 < chunks:
            stage_back(step - 2)
    shifted_out[...] = panel[...]

    @pl.when(row == 0)
    def _():
        shifted_out[:PANEL] = panel[:PANEL] + factor
        for k in range(chunks):
            for r in range(1, n_row):
                scatter(k, r).wait_send()

    for k in range(chunks):
        mirror = hold.at[:, columns(k, other)]
        send(mirror, mirror, back_send.at[k], back_recv.at[k], partner).wait_recv()
    for k in range(chunks):
        pair(k).wait_send()
        back(k).wait_send()
        for d in range(1, outer_n):
            far(k, d).wait_send()
            done(k, d).wait_send()


def whole_step(matrix, n_row, n_col):
    height, width = matrix.shape
    piece = PANEL // n_row
    inner_n = 2
    outer_n = n_row // inner_n
    chunks = width // (n_row * LANES)
    span = outer_n * LANES
    dma = pltpu.SemaphoreType.DMA
    f32 = jnp.float32
    return pl.pallas_call(
        functools.partial(step_kernel, n_row, n_col, inner_n, chunks),
        out_shape=(jax.ShapeDtypeStruct((height, PANEL), f32), jax.ShapeDtypeStruct((PANEL, width), f32)),
        in_specs=[pl.BlockSpec(memory_space=pl.ANY)],
        out_specs=(pl.BlockSpec(memory_space=pltpu.VMEM),) * 2,
        scratch_shapes=[
            pltpu.VMEM((height, width), f32),
            pltpu.VMEM((PANEL, width), f32),
            pltpu.VMEM((2 * PANEL, height), jnp.bfloat16),
            pltpu.VMEM((chunks, PANEL, span), f32),
            pltpu.VMEM((chunks, outer_n, PANEL, LANES), f32),
            pltpu.VMEM((chunks, outer_n - 1, PANEL, LANES), f32),
            pltpu.VMEM((chunks, PANEL, LANES), f32),
            pltpu.VMEM((height, PANEL), f32),
            pltpu.VMEM((PANEL, PANEL), f32),
            pltpu.VMEM((n_row, piece, PANEL), f32),
            pltpu.VMEM((n_row - 1, piece, PANEL), f32),
            pltpu.VMEM((n_row, piece, PANEL), f32),
            dma((2,)),
            dma((chunks,)),
            dma((chunks,)),
            dma((n_col - 1,)),
            dma((n_row - 1,)),
            dma((n_row - 1,)),
            dma((n_row - 1,)),
            dma((2 * n_col - 2,)),
            dma((chunks, n_row - 1)),
            dma((1,)),
            dma((1,)),
            dma((n_row - 1,)),
            dma((n_row - 1,)),
            dma((2,)),
            dma((chunks,)),
            dma((chunks,)),
            dma((chunks, outer_n - 1)),
            dma((chunks, outer_n - 1)),
            dma((chunks,)),
            dma((chunks,)),
            dma((chunks, outer_n - 1)),
            dma((chunks, outer_n - 1)),
            dma((chunks,)),
        ],
        compiler_params=pltpu.CompilerParams(
            collective_id=0, has_side_effects=True, vmem_limit_bytes=48 * 1024 * 1024
        ),
        name="whole_step",
    )(matrix)


def on_device(n_row, n_col, matrix):
    shifted, coefficients = whole_step(matrix, n_row, n_col)
    return matrix - jnp.dot(shifted, coefficients, precision=lax.Precision.HIGH)


def solution(mesh):
    body = functools.partial(on_device, mesh.shape["row"], mesh.shape["col"])
    return jax.shard_map(body, mesh=mesh, in_specs=(P("row", "col"),), out_specs=P("row", "col"), check_vma=False)
```

```python
import functools

import jax
import jax.numpy as jnp
from jax import lax
from jax.experimental import pallas as pl
from jax.experimental.pallas import tpu as pltpu
from jax.sharding import PartitionSpec as P

PANEL = 128
STRIP = 8
LANES = 128
MESH = pl.DeviceIdType.MESH


def dot_exact(a, b, contract):
    return lax.dot_general(
        a, b, (contract, ((), ())), precision=lax.Precision.HIGHEST, preferred_element_type=jnp.float32
    )


def factor_values(gram, top, between=lambda strip: None):
    strips = PANEL // STRIP
    rows = lax.broadcasted_iota(jnp.int32, (STRIP, 1), 0)
    eye = (
        lax.broadcasted_iota(jnp.int32, (PANEL, PANEL), 0) == lax.broadcasted_iota(jnp.int32, (PANEL, PANEL), 1)
    ).astype(jnp.float32)
    chol = jnp.concatenate([gram, eye], axis=1)
    work = jnp.concatenate([top, jnp.zeros_like(top)], axis=1)
    factor_rows = []
    lanes = lax.broadcasted_iota(jnp.int32, (STRIP, 2 * PANEL), 1)
    previous = None
    for strip in range(strips + 1):
        at, back = strip * STRIP, (strip - 1) * STRIP
        if strip < strips:
            between(strip)
            panel = chol[:STRIP]
            scale = jnp.ones((STRIP, 1), jnp.float32)
        if strip > 0:
            inner = work[back : back + STRIP] + previous
            aside = work[:, back : back + STRIP]
        for j in range(STRIP):
            if strip < strips:
                column = panel[:, at + j : at + j + 1]
                pivot = column[j : j + 1]
                multiplier = jnp.where(rows > j, column / pivot, 0.0)
            if strip > 0:
                inner_column = inner[:, back + j : back + j + 1]
                pivot_row = inner[j : j + 1] / inner_column[j : j + 1]
            if strip < strips:
                scale = jnp.where(rows == j, lax.rsqrt(pivot), scale)
                panel = panel - multiplier * panel[j : j + 1]
            if strip > 0:
                inner = jnp.where(rows == j, pivot_row, inner - inner_column * pivot_row)
        if strip < strips:
            panel = jnp.where(lanes >= at + rows, panel * scale, 0.0)
            factor_rows.append(panel[:, :PANEL])
            if strip < strips - 1:
                chol = chol[STRIP:] - dot_exact(panel[:, at + STRIP : PANEL], panel, ((0,), (0,)))
        if strip > 0:
            update = dot_exact(aside, inner, ((1,), (0,)))
            pieces = []
            if back > 0:
                pieces.append(work[:back] - update[:back])
            pieces.append(inner)
            if strip < strips:
                pieces.append(work[at:] - update[at:])
            work = jnp.concatenate(pieces, axis=0)
        previous = panel
    return jnp.concatenate(factor_rows, axis=0), work[:, PANEL:]


def everyone_ready(n_row, n_col):
    row, col = lax.axis_index("row"), lax.axis_index("col")
    barrier = pltpu.get_barrier_semaphore()
    for d in range(1, n_row):
        pl.semaphore_signal(barrier, inc=1, device_id={"row": lax.rem(row + d, n_row)}, device_id_type=MESH)
    for d in range(1, n_col):
        pl.semaphore_signal(barrier, inc=1, device_id={"col": lax.rem(col + d, n_col)}, device_id_type=MESH)
    pl.semaphore_wait(barrier, n_row - 1 + max(n_col - 1, 0))


def send(src, dst, send_sem, recv_sem, target):
    return pltpu.make_async_remote_copy(
        src_ref=src, dst_ref=dst, send_sem=send_sem, recv_sem=recv_sem, device_id=target, device_id_type=MESH
    )


def split(x):
    high = x.astype(jnp.bfloat16)
    return high, (x - high.astype(jnp.float32)).astype(jnp.bfloat16)


def step_kernel(
    n_row, n_col, inner_n, chunks, matrix_ref, shifted_out, hold,
    block, partial, stacked, pair_in, half, far_in, top_in, panel, top, parts, arrived, whole,
    local_sem, block_sem, own_sem,
    panel_send, top_send, part_send, whole_send, share_send, scatter_send,
    panel_recv, top_recv, part_recv, whole_recv, share_recv, scatter_recv,
    pair_send, far_send, done_send, back_send, pair_recv, far_recv, done_recv, back_recv,
):
    row, col = lax.axis_index("row"), lax.axis_index("col")
    piece = PANEL // n_row
    outer_n = n_row // inner_n
    outer, inner = row // inner_n, lax.rem(row, inner_n)
    other = 1 - inner
    partner = {"row": outer * inner_n + other}
    span = outer_n * LANES
    everyone_ready(n_row, n_col)

    def load(k):
        place = pl.ds(k * inner_n * span, inner_n * span)
        return pltpu.make_async_copy(matrix_ref.at[:, place], block.at[:, place], block_sem.at[k])

    def scatter(k, r):
        place = pl.ds((k * inner_n + r % inner_n) * span + r // inner_n * LANES, LANES)
        return send(
            matrix_ref.at[pl.ds(0, PANEL), place], top_in.at[k],
            scatter_send.at[k, r - 1], scatter_recv.at[k], {"row": r},
        )

    def keep(k):
        place = pl.ds(k * inner_n * span, LANES)
        return pltpu.make_async_copy(matrix_ref.at[pl.ds(0, PANEL), place], top_in.at[k], own_sem.at[k])

    def start_scatter():
        for k in range(chunks):
            for r in range(1, n_row):
                scatter(k, r).start()
            keep(k).start()

    def columns(k, i):
        return pl.ds(pl.multiple_of((k * inner_n + i) * span, span), span)

    def peer(d):
        return lax.rem(outer + d, outer_n)

    def pair(k):
        return send(partial.at[:, columns(k, other)], pair_in.at[k], pair_send.at[k], pair_recv.at[k], partner)

    def far(k, d):
        q = peer(d)
        return send(
            half.at[k, q], far_in.at[k, d - 1], far_send.at[k, d - 1], far_recv.at[k, d - 1],
            {"row": q * inner_n + inner},
        )

    def spot(k, o):
        return pl.ds(pl.multiple_of((k * inner_n + inner) * span + o * LANES, LANES), LANES)

    def done(k, d):
        return send(
            hold.at[:, spot(k, outer)], hold.at[:, spot(k, outer)], done_send.at[k, d - 1], done_recv.at[k, d - 1],
            {"row": peer(d) * inner_n + inner},
        )

    def back(k):
        return send(hold.at[:, columns(k, inner)], hold.at[:, columns(k, inner)], back_send.at[k], back_recv.at[k], partner)

    def multiply(k, i):
        place = columns(k, i)
        high, low = split(block[:, place])
        both = jnp.dot(stacked[...], high, preferred_element_type=jnp.float32)
        rest = jnp.dot(stacked[:PANEL], low, preferred_element_type=jnp.float32)
        partial[:, place] = both[:PANEL] + both[PANEL:] + rest

    def prepare():
        for k in range(chunks):
            load(k).wait()
        high, low = split(jnp.transpose(panel[...]))
        stacked[:PANEL] = high
        stacked[PANEL:] = low

    @pl.when((row == 0) & (col != 0))
    def _():
        start_scatter()

    @pl.when(col == 0)
    def _():
        fetch = pltpu.make_async_copy(matrix_ref.at[:, pl.ds(0, PANEL)], panel, local_sem.at[0])
        fetch.start()
        fetch.wait()
        for k in range(chunks):
            load(k).start()
        panel_copies = [
            send(panel, panel, panel_send.at[c - 1], panel_recv.at[0], {"col": c}) for c in range(1, n_col)
        ]

        @pl.when(row == 0)
        def _():
            for r in range(1, n_row):
                send(panel.at[pl.ds(0, PANEL)], top, top_send.at[r - 1], top_recv.at[0], {"row": r}).start()
            own = pltpu.make_async_copy(panel.at[pl.ds(0, PANEL)], top, local_sem.at[1])
            own.start()
            own.wait()

        local = dot_exact(panel[...], panel[...], ((0,), (0,)))
        for q in range(n_row):
            parts[q] = local[q * piece : (q + 1) * piece]
        part_copies = []
        for d in range(1, n_row):
            q = lax.rem(row + d, n_row)
            part_copies.append(
                send(parts.at[q], arrived.at[d - 1], part_send.at[d - 1], part_recv.at[d - 1], {"row": q})
            )
            part_copies[-1].start()
        for copy in panel_copies:
            copy.start()
        prepare()
        early = min(2, chunks)
        for k in range(early):
            multiply(k, other)
        total = parts[row]
        for d in range(1, n_row):
            part_copies[d - 1].wait_recv()
            total = total + arrived[d - 1]
        whole[row] = total
        whole_copies = []
        for d in range(1, n_row):
            q = lax.rem(row + d, n_row)
            whole_copies.append(
                send(whole.at[row], whole.at[row], whole_send.at[d - 1], whole_recv.at[d - 1], {"row": q})
            )
            whole_copies[-1].start()
        for k in range(early, chunks):
            multiply(k, other)
        for k in range(chunks):
            pair(k).start()

        @pl.when(row == 0)
        def _():
            start_scatter()

        @pl.when(row != 0)
        def _():
            send(top, top, top_send.at[0], top_recv.at[0], {"row": 0}).wait_recv()

        for d in range(1, n_row):
            q = lax.rem(row - d + n_row, n_row)
            send(whole.at[q], whole.at[q], whole_send.at[d - 1], whole_recv.at[d - 1], {"row": q}).wait_recv()
        shares = []
        for c in range(1, n_col):
            shares.append(send(top, top, share_send.at[2 * c - 2], share_recv.at[0], {"col": c}))
            shares.append(send(whole, whole, share_send.at[2 * c - 1], share_recv.at[1], {"col": c}))
        for copy in shares:
            copy.start()

        @pl.when(row == 0)
        def _():
            for r in range(1, n_row):
                send(panel.at[pl.ds(0, PANEL)], top, top_send.at[r - 1], top_recv.at[0], {"row": r}).wait_send()

        for copy in part_copies + panel_copies + whole_copies + shares:
            copy.wait_send()

    @pl.when(col != 0)
    def _():
        for k in range(chunks):
            load(k).start()
        root = {"col": 0}
        send(panel, panel, panel_send.at[0], panel_recv.at[0], root).wait_recv()
        prepare()
        for k in range(chunks):
            multiply(k, other)
            pair(k).start()
        send(top, top, share_send.at[0], share_recv.at[0], root).wait_recv()
        send(whole, whole, share_send.at[1], share_recv.at[1], root).wait_recv()

    def stage_far(k):
        pair(k).wait_recv()
        for o in range(outer_n):
            half[k, o] = partial[:, spot(k, o)] + pair_in[k, :, o * LANES : (o + 1) * LANES]
        for d in range(1, outer_n):
            far(k, d).start()

    def stage_done(k, factor, inverse):
        total = half[k, outer]
        for d in range(1, outer_n):
            far(k, d).wait_recv()
            total = total + far_in[k, d - 1]

        @pl.when(row == 0)
        def _():
            keep(k).wait()

        @pl.when(row != 0)
        def _():
            send(top_in.at[k], top_in.at[k], scatter_send.at[k, 0], scatter_recv.at[k], {"row": 0}).wait_recv()

        total = total + dot_exact(factor, top_in[k], ((0,), (0,)))
        hold[:, spot(k, outer)] = dot_exact(inverse, total, ((1,), (0,)))
        for d in range(1, outer_n):
            done(k, d).start()

    def stage_back(k):
        for d in range(1, outer_n):
            q = lax.rem(outer - d + outer_n, outer_n)
            send(
                hold.at[:, spot(k, q)], hold.at[:, spot(k, q)], done_send.at[k, d - 1], done_recv.at[k, d - 1],
                {"row": q * inner_n + inner},
            ).wait_recv()
        back(k).start()

    gram = jnp.concatenate([whole[q] for q in range(n_row)], axis=0)

    def between(strip):
        if strip < chunks:
            multiply(strip, inner)
        elif strip >= first_far and (strip - first_far) % 3 == 0 and (strip - first_far) // 3 < ready:
            stage_far((strip - first_far) // 3)

    first_far = 2 * chunks
    ready = max(0, min(chunks - 1, (PANEL // STRIP - first_far + 2) // 3))
    factor, inverse = factor_values(gram, top[...], between)
    for step in range(chunks + 2):
        if step < ready:
            stage_done(step, factor, inverse)
        if ready + step < chunks:
            stage_far(ready + step)
        if ready <= step < chunks:
            stage_done(step, factor, inverse)
        if 0 <= step - 2 < chunks:
            stage_back(step - 2)
    shifted_out[...] = panel[...]

    @pl.when(row == 0)
    def _():
        shifted_out[:PANEL] = panel[:PANEL] + factor
        for k in range(chunks):
            for r in range(1, n_row):
                scatter(k, r).wait_send()

    for k in range(chunks):
        mirror = hold.at[:, columns(k, other)]
        send(mirror, mirror, back_send.at[k], back_recv.at[k], partner).wait_recv()
    for k in range(chunks):
        pair(k).wait_send()
        back(k).wait_send()
        for d in range(1, outer_n):
            far(k, d).wait_send()
            done(k, d).wait_send()


def whole_step(matrix, n_row, n_col):
    height, width = matrix.shape
    piece = PANEL // n_row
    inner_n = 2
    outer_n = n_row // inner_n
    chunks = width // (n_row * LANES)
    span = outer_n * LANES
    dma = pltpu.SemaphoreType.DMA
    f32 = jnp.float32
    return pl.pallas_call(
        functools.partial(step_kernel, n_row, n_col, inner_n, chunks),
        out_shape=(jax.ShapeDtypeStruct((height, PANEL), f32), jax.ShapeDtypeStruct((PANEL, width), f32)),
        in_specs=[pl.BlockSpec(memory_space=pl.ANY)],
        out_specs=(pl.BlockSpec(memory_space=pltpu.VMEM),) * 2,
        scratch_shapes=[
            pltpu.VMEM((height, width), f32),
            pltpu.VMEM((PANEL, width), f32),
            pltpu.VMEM((2 * PANEL, height), jnp.bfloat16),
            pltpu.VMEM((chunks, PANEL, span), f32),
            pltpu.VMEM((chunks, outer_n, PANEL, LANES), f32),
            pltpu.VMEM((chunks, outer_n - 1, PANEL, LANES), f32),
            pltpu.VMEM((chunks, PANEL, LANES), f32),
            pltpu.VMEM((height, PANEL), f32),
            pltpu.VMEM((PANEL, PANEL), f32),
            pltpu.VMEM((n_row, piece, PANEL), f32),
            pltpu.VMEM((n_row - 1, piece, PANEL), f32),
            pltpu.VMEM((n_row, piece, PANEL), f32),
            dma((2,)),
            dma((chunks,)),
            dma((chunks,)),
            dma((n_col - 1,)),
            dma((n_row - 1,)),
            dma((n_row - 1,)),
            dma((n_row - 1,)),
            dma((2 * n_col - 2,)),
            dma((chunks, n_row - 1)),
            dma((1,)),
            dma((1,)),
            dma((n_row - 1,)),
            dma((n_row - 1,)),
            dma((2,)),
            dma((chunks,)),
            dma((chunks,)),
            dma((chunks, outer_n - 1)),
            dma((chunks, outer_n - 1)),
            dma((chunks,)),
            dma((chunks,)),
            dma((chunks, outer_n - 1)),
            dma((chunks, outer_n - 1)),
            dma((chunks,)),
        ],
        compiler_params=pltpu.CompilerParams(
            collective_id=0, has_side_effects=True, vmem_limit_bytes=48 * 1024 * 1024
        ),
        name="whole_step",
    )(matrix)


def on_device(n_row, n_col, matrix):
    shifted, coefficients = whole_step(matrix, n_row, n_col)
    return matrix - jnp.dot(shifted, coefficients, precision=lax.Precision.HIGH)


def solution(mesh):
    body = functools.partial(on_device, mesh.shape["row"], mesh.shape["col"])
    return jax.shard_map(body, mesh=mesh, in_specs=(P("row", "col"),), out_specs=P("row", "col"), check_vma=False)
```
